32 devices in a mesh: dp: 8 (over z, core), expert: 4 (over y, x).
Axes of the slice: x: 2, y: 2, z: 4, core: 2. Of those that a mesh axis runs over, the one named last changes fastest.
Arguments:
- tokens: bfloat16 [4096, 2048], P(('dp', 'expert')), may hold values from -6 to 6
- out_grad: bfloat16 [4096, 2048], P(('dp', 'expert')), may hold values from -1.5 to 1.5
- routes: int32 [4096, 2], P(('dp', 'expert')), may hold values from 0 to 3, all different within a row; in each aligned block of 128 rows (0 to 127, 128 to 255, ...) at most 128 rows name the same one
- route_probs: bfloat16 [4096, 2], P(('dp', 'expert')), may hold values from 0.049804688 to 1
- kept_count: int32 [8], P('dp'), may hold values from 128 to 512, as said below
- gate_weight: bfloat16 [4, 2048, 768], P('expert', 'dp'), may hold values from -0.125 to 0.125
- up_weight: bfloat16 [4, 2048, 768], P('expert', 'dp'), may hold values from -0.125 to 0.125
- down_weight: bfloat16 [4, 2048, 768], P('expert', 'dp'), may hold values from -0.21875 to 0.21875
Outputs:
- token_grad: bfloat16 [4096, 2048], P(('dp', 'expert'))
- prob_grad: bfloat16 [4096, 2], P(('dp', 'expert'))
- weight_grad: bfloat16 [4, 2048, 2304], P('expert', 'dp')
The draws below stay inside these ranges and needn't reach their ends.
Inputs may be any that keep to these rules, and one draw needn't show every extreme that they name: `routes`: among the rows of one device, no expert is named more than 128 times, and a row names 2 different experts. `kept_count`: rows of a data group whose index within the group is below its count are kept; in every draw some group keeps all its rows and another keeps a quarter of them.
All inputs are finite; a program needn't handle non-finite values.
Results may differ from the reference program's by a relative error of at most 0.018.
Values may be sent and summed in bfloat16 or wider, within the bound.
A program may use at most 128 MiB of HBM per device.

```python
import math
import jax
import jax.numpy as jnp
import numpy as np
from jax import lax

D = 2048
FF = 768
TOP = 2
TOK_DEV = 128
EXPERTS = 4
CAP = 128
GROUP_ROWS = 512
TOKENS = 4096
N_DP = 8
N_EXPERT = 4


def draw_kept_count(key, part):
    counts = jax.random.randint(jax.random.fold_in(key, 11), (N_DP,), GROUP_ROWS // 4, GROUP_ROWS + 1).astype(jnp.int32)
    order = jax.random.permutation(jax.random.fold_in(key, 12), N_DP)
    counts = counts.at[order[0]].set(GROUP_ROWS)
    counts = counts.at[order[1]].set(GROUP_ROWS // 4)
    return counts.astype(jnp.int32)


def steps_of(key, dims, shards, low, top_value):
    level, own = 1.0, jax.random.fold_in(key, 6)
    for axis_at, parts in shards:
        heights = jnp.exp(jax.random.uniform(jax.random.fold_in(own, axis_at), (parts,), jnp.float32, low / len(shards), top_value / len(shards)))
        level = level * jnp.repeat(heights, dims[axis_at] // parts).reshape([-1 if axis == axis_at else 1 for axis in range(len(dims))])
    return level


def routed_block(own_key, own, number, rows, amount, top, limit, slope):
    sequence = jax.random.permutation(own_key, amount)
    crowded, common = shares(amount, rows * top, limit, slope, True), shares(amount, rows * top, limit, slope, False)
    places = jnp.arange(amount)

    def named(tallies, turn):
        used = int((tallies > 0).sum())
        fixed = max(1, used // 4)
        passed = fixed + (places - fixed + turn * (used - fixed)) % max(1, amount - fixed)
        return jnp.zeros((amount,), jnp.int32).at[sequence[jnp.where(places < fixed, places, passed)]].set(jnp.asarray(tallies, jnp.int32))

    tallies = jnp.where(number % 4 == 0, named(crowded, number // 4), named(common, number - number // 4 - 1))
    mixed = jax.random.permutation(jax.random.fold_in(own, 3), amount)
    donor, sink = mixed[0:amount // 2 * 2:2], mixed[1:amount // 2 * 2:2]
    slack = jnp.minimum(tallies[donor] - 1, limit - tallies[sink]) // 2
    slack = jnp.where((donor == sequence[0]) | (sink == sequence[0]) | (tallies[sink] == 0), 0, jnp.maximum(slack, 0))
    passed = jax.random.randint(jax.random.fold_in(own, 4), (amount // 2,), 0, 1 << 20) % (slack + 1)
    tallies = tallies.at[donor].add(-passed).at[sink].add(passed)
    members = jnp.searchsorted(jnp.cumsum(tallies), jnp.arange(rows * top), side="right").astype(jnp.int32)
    listing = members.reshape(top, rows).T
    listing = listing[jax.random.permutation(jax.random.fold_in(own, 1), rows)]
    turn = jax.random.randint(jax.random.fold_in(own, 2), (rows, 1), 0, top)
    return jnp.take_along_axis(listing, (jnp.arange(top)[None, :] + turn) % top, axis=1)


def shares(number_of, total, limit, lean, full):
    loads = [(1 << 20) // math.isqrt(grade ** lean) + 1 for grade in range(1, number_of + 1)]
    largest = limit if full else min(limit, max(-(-total // number_of), total * loads[0] // sum(loads)))
    least = 1 if total - largest >= number_of - 1 else 0
    holding, spare = [largest] + [least] * (number_of - 1), total - largest - least * (number_of - 1)
    while spare > 0:
        free = [i for i in range(1, number_of) if holding[i] < largest] or [i for i in range(1, number_of) if holding[i] < limit]
        mass, budget = sum([loads[i] for i in free]), spare
        for i in free:
            more = min(limit - holding[i], max(1, budget * loads[i] // mass), spare)
            holding[i] = holding[i] + more
            spare = spare - more
    return np.array(holding)


def bell_draw(rng, extent, deviation, reach, pieces=(), held_as=jnp.bfloat16):
    drawn = deviation * jax.random.normal(rng, extent, jnp.float32)
    if pieces:
        drawn = drawn * steps_of(rng, extent, pieces, -0.22, 0.18)
    return jnp.clip(drawn, -reach, reach).astype(held_as)


def setup_inputs(seed: int = 0) -> dict:
    arg_keys = jax.random.split(jax.random.key(seed), 9)
    tokens = bell_draw(arg_keys[0], (TOKENS, D), 1.0, 6.0, ((0, 32),))
    out_grad = bell_draw(arg_keys[1], (TOKENS, D), 0.25, 1.5, ((0, 32),))
    routes_keys = jax.random.split(jax.random.fold_in(arg_keys[2], 1), TOKENS // TOK_DEV)
    routes_turns = jax.random.permutation(jax.random.fold_in(arg_keys[2], 3), TOKENS // TOK_DEV)
    routes = jax.vmap(lambda own, number: routed_block(jax.random.fold_in(arg_keys[2], 2), own, number, TOK_DEV, EXPERTS, TOP, CAP, 2))(routes_keys, routes_turns).reshape((TOKENS, TOP))
    route_probs = jnp.clip(jnp.exp(math.log(1.0) - 2.9996462 * jax.random.uniform(arg_keys[3], (TOKENS, TOP), jnp.float32) ** steps_of(arg_keys[3], (TOKENS, TOP), ((0, 32),), -0.2, 0.2)), 0.049804688, 1.0).astype(jnp.bfloat16)
    kept_count = draw_kept_count(jax.random.fold_in(arg_keys[8], 71), 0)
    gate_weight = bell_draw(arg_keys[5], (EXPERTS, D, FF), D ** -0.5, 0.125, ((0, 4), (1, 8)))
    up_weight = bell_draw(arg_keys[6], (EXPERTS, D, FF), D ** -0.5, 0.125, ((0, 4), (1, 8)))
    down_weight = bell_draw(arg_keys[7], (EXPERTS, D, FF), FF ** -0.5, 0.21875, ((0, 4), (1, 8)))
    return {"tokens": tokens, "out_grad": out_grad, "routes": routes, "route_probs": route_probs, "kept_count": kept_count, "gate_weight": gate_weight, "up_weight": up_weight, "down_weight": down_weight}


def slot_positions(routes):
    blocks = routes.reshape(N_DP * N_EXPERT, TOK_DEV * TOP)
    onehot = (blocks[:, :, None] == jnp.arange(EXPERTS, dtype=jnp.int32)[None, None, :]).astype(jnp.int32)
    before = jnp.cumsum(onehot, axis=1) - onehot
    position = jnp.sum(before * onehot, axis=2)
    return position.reshape(TOKENS, TOP).astype(jnp.int32)


def reference(tokens, out_grad, routes, route_probs, kept_count, gate_weight, up_weight, down_weight):
    row = jnp.arange(TOKENS, dtype=jnp.int32)
    kept = (row % GROUP_ROWS) < kept_count[row // GROUP_ROWS]
    masked = jnp.where(kept[:, None], out_grad, jnp.zeros_like(out_grad))
    position = slot_positions(routes)
    block = row // TOK_DEV
    group = (block // N_EXPERT).astype(jnp.int32)
    source = (block % N_EXPERT).astype(jnp.int32)
    route_id = (row[:, None] * TOP + jnp.arange(TOP, dtype=jnp.int32)[None, :]).astype(jnp.int32)
    empty_id = TOKENS * TOP
    table = jnp.full((EXPERTS, N_DP, N_EXPERT, CAP), empty_id, jnp.int32)
    table = table.at[routes, group[:, None], source[:, None], position].set(route_id)
    flat_probs = route_probs.reshape(-1)

    def expert_step(carry, inputs):
        contrib, prob_acc = carry
        ids, w_gate, w_up, w_down = inputs
        ids = ids.reshape(-1)
        valid = ids < empty_id
        safe = jnp.where(valid, ids, 0).astype(jnp.int32)
        token_of = (safe // TOP).astype(jnp.int32)
        rows_in = jnp.where(valid[:, None], tokens[token_of], jnp.zeros((), jnp.bfloat16))
        grad_in = jnp.where(valid[:, None], masked[token_of], jnp.zeros((), jnp.bfloat16))
        prob_in = jnp.where(valid, flat_probs[safe], jnp.zeros((), jnp.bfloat16))
        pre_gate = jnp.dot(rows_in, w_gate, preferred_element_type=jnp.float32)
        pre_up = jnp.dot(rows_in, w_up, preferred_element_type=jnp.float32)
        sig = jax.nn.sigmoid(pre_gate)
        act = (pre_gate * sig * pre_up).astype(jnp.bfloat16)
        output_rows = jnp.dot(act, w_down.T, preferred_element_type=jnp.float32)
        prob_part = jnp.sum(grad_in.astype(jnp.float32) * output_rows, axis=1).astype(jnp.bfloat16)
        scaled = (prob_in.astype(jnp.float32)[:, None] * grad_in.astype(jnp.float32)).astype(jnp.bfloat16)
        back_hidden = jnp.dot(scaled, w_down, preferred_element_type=jnp.float32)
        d_gate = (back_hidden * pre_up * sig * (1.0 + pre_gate * (1.0 - sig))).astype(jnp.bfloat16)
        d_up = (back_hidden * pre_gate * sig).astype(jnp.bfloat16)
        route_back = (jnp.dot(d_gate, w_gate.T, preferred_element_type=jnp.float32)
                      + jnp.dot(d_up, w_up.T, preferred_element_type=jnp.float32)).astype(jnp.bfloat16)
        rows_g = rows_in.reshape(N_DP, N_EXPERT * CAP, D).astype(jnp.float32)
        scaled_g = scaled.reshape(N_DP, N_EXPERT * CAP, D).astype(jnp.float32)
        gate_g = d_gate.reshape(N_DP, N_EXPERT * CAP, FF).astype(jnp.float32)
        up_g = d_up.reshape(N_DP, N_EXPERT * CAP, FF).astype(jnp.float32)
        act_g = act.reshape(N_DP, N_EXPERT * CAP, FF).astype(jnp.float32)
        partial_value = jnp.concatenate((jnp.einsum('grd,grf->gdf', rows_g, gate_g),
                                   jnp.einsum('grd,grf->gdf', rows_g, up_g),
                                   jnp.einsum('grd,grf->gdf', scaled_g, act_g)), axis=2).astype(jnp.bfloat16)
        summed = jnp.sum(partial_value.astype(jnp.float32), axis=0).astype(jnp.bfloat16)
        contrib = contrib.at[ids].set(route_back, mode="drop")
        prob_acc = prob_acc.at[ids].set(prob_part, mode="drop")
        return (contrib, prob_acc), summed

    start = (jnp.zeros((TOKENS * TOP, D), jnp.bfloat16), jnp.zeros((TOKENS * TOP,), jnp.bfloat16))
    (contrib, prob_acc), weight_grad = lax.scan(expert_step, start, (table, gate_weight, up_weight, down_weight))
    token_grad = jnp.sum(contrib.reshape(TOKENS, TOP, D).astype(jnp.float32), axis=1).astype(jnp.bfloat16)
    prob_grad = prob_acc.reshape(TOKENS, TOP)
    return token_grad, prob_grad, weight_grad
```

```python
import jax
import jax.numpy as jnp
from jax import lax
from jax.sharding import PartitionSpec as P
from jax.experimental import pallas as pl
from jax.experimental.pallas import tpu as pltpu

MESH = pl.DeviceIdType.MESH
CORES = 2


def dot_f32(left, right):
    return jnp.dot(left, right, preferred_element_type=jnp.float32)


def contract_rows(left, right):
    return lax.dot_general(
        left, right, (((0,), (0,)), ((), ())), preferred_element_type=jnp.float32
    )


def contract_last(left, right):
    return lax.dot_general(
        left, right, (((1,), (1,)), ((), ())), preferred_element_type=jnp.float32
    )


def hop(x, axis, mask, name):
    size = lax.axis_size(axis)
    with jax.named_scope(name):
        return lax.ppermute(x, axis, [(i, i ^ mask) for i in range(size)])


def z_send(x, moves, name):
    pairs = [(a * CORES + c, b * CORES + c) for a, b in moves for c in range(CORES)]
    with jax.named_scope(name):
        return lax.ppermute(x, "dp", pairs)


def xor_blocks(x, blocks):
    me = lax.axis_index("dp")
    rows, width = x.shape
    size = width // blocks
    depth = blocks // CORES
    parts = [x[:, i * size : (i + 1) * size] for i in range(blocks)]
    bit = 1
    while bit < blocks:
        flip = (me & bit) != 0
        parts = [jnp.where(flip, parts[i ^ bit], parts[i]) for i in range(blocks)]
        bit *= 2
    return parts, depth


def to_local(x, blocks):
    parts, depth = xor_blocks(x, blocks)
    return jnp.concatenate([parts[kz * CORES + kc] for kc in range(CORES) for kz in range(depth)], 1)


def from_local(x, blocks):
    depth = blocks // CORES
    size = x.shape[1] // blocks
    cut = [x[:, i * size : (i + 1) * size] for i in range(blocks)]
    natural = [cut[kc * depth + kz] for kz in range(depth) for kc in range(CORES)]
    parts, _ = xor_blocks(jnp.concatenate(natural, 1), blocks)
    return jnp.concatenate(parts, 1)


def spread(x, experts, name):
    if experts != 4:
        return jnp.concatenate([x] + [hop(x, "expert", k, f"{name}{k}") for k in range(1, experts)], 0)
    half = x.shape[0] // 2
    along_x = hop(x, "expert", 1, f"{name}_x")
    along_y = hop(x, "expert", 2, f"{name}_y")
    top = hop(along_x[:half], "expert", 2, f"{name}_xy")
    bottom = hop(along_y[half:], "expert", 1, f"{name}_yx")
    return jnp.concatenate([x, along_x, along_y, top, bottom], 0)


def reduce_line(q, depth, tag):
    def add(a, b):
        return (a.astype(jnp.float32) + b.astype(jnp.float32)).astype(jnp.bfloat16)

    if depth != 4:
        total = q[0].astype(jnp.float32)
        for kz in range(1, depth):
            total = total + hop(q[kz], "dp", kz * CORES, f"{tag}_{kz}").astype(jnp.float32)
        return total.astype(jnp.bfloat16)
    outer, middle, inner = [(3, 2), (0, 1)], [(2, 1), (1, 2)], [(1, 0), (2, 3)]
    a0 = z_send(q[3], outer, f"{tag}_a0")
    a1 = z_send(q[2], outer, f"{tag}_a1")
    a2 = z_send(q[1], outer, f"{tag}_a2")
    b0 = z_send(add(q[2], a0), middle, f"{tag}_b0")
    b1 = z_send(add(q[3], a1), middle, f"{tag}_b1")
    c0 = z_send(add(q[1], b0), inner, f"{tag}_c0")
    total = q[0].astype(jnp.float32) + a2.astype(jnp.float32)
    return (total + b1.astype(jnp.float32) + c0.astype(jnp.float32)).astype(jnp.bfloat16)


def gather_line(own, depth, tag):
    if depth != 4:
        return jnp.concatenate(
            [own] + [hop(own, "dp", kz * CORES, f"{tag}_{kz}") for kz in range(1, depth)], 0
        )
    z = lax.axis_index("dp") // CORES
    inside = (z == 1) | (z == 2)
    outer, middle, inner = [(3, 2), (0, 1)], [(2, 1), (1, 2)], [(1, 0), (2, 3)]
    o = z_send(own, outer, f"{tag}_o")
    m0 = z_send(own, middle, f"{tag}_m0")
    i0 = z_send(own, inner, f"{tag}_i0")
    m1 = z_send(o, middle, f"{tag}_m1")
    i1 = z_send(m0, inner, f"{tag}_i1")
    i2 = z_send(m1, inner, f"{tag}_i2")
    return jnp.concatenate(
        [own, jnp.where(inside, o, i0), jnp.where(inside, m1, i1), jnp.where(inside, m0, i2)], 0
    )


def chunks_of(hidden):
    return 3 if hidden % 384 == 0 else 1


def per_device(
    tokens, out_grad, routes, route_probs, kept_count, gate_weight, up_weight, down_weight
):
    tok_rows, width = tokens.shape
    experts = lax.axis_size("expert")
    groups = lax.axis_size("dp")
    depth = groups // CORES
    hidden = gate_weight.shape[2]
    count = chunks_of(hidden)
    step = hidden // count
    me = lax.axis_index("expert")

    row = me * tok_rows + jnp.arange(tok_rows, dtype=jnp.int32)
    kept = row < kept_count[0]
    masked = jnp.where(kept[:, None], out_grad, jnp.zeros_like(out_grad))
    probs = route_probs.astype(jnp.float32)

    def share(k):
        return jnp.sum(jnp.where(routes == (me ^ k), probs, 0.0), axis=1)

    prob_in = jnp.concatenate(
        [share(0)] + [hop(share(k)[None], "expert", k, f"prob{k}")[0] for k in range(1, experts)]
    )
    rows_in = spread(to_local(tokens, groups), experts, "rows")
    grad_in = spread(to_local(masked, groups), experts, "grad")

    half = width // CORES
    scores = 0.0
    back = [0.0, 0.0]
    sums = []
    for j in range(count):
        cut = slice(j * step, (j + 1) * step)
        own = jnp.concatenate(
            [gate_weight[0][:, cut], up_weight[0][:, cut], down_weight[0][:, cut]], 1
        )
        mine = gather_line(own, depth, f"g{j}")
        other = hop(mine, "dp", 1, f"pair{j}")
        both = (mine, other)
        pre = sum(dot_f32(rows_in[:, i * half : (i + 1) * half], both[i][:, : 2 * step]) for i in range(2))
        cot = sum(dot_f32(grad_in[:, i * half : (i + 1) * half], both[i][:, 2 * step :]) for i in range(2))
        a, b = pre[:, :step], pre[:, step:]
        sig = jax.nn.sigmoid(a)
        act = a * sig * b
        act_low = act.astype(jnp.bfloat16).astype(jnp.float32)
        scores = scores + jnp.sum(act_low * cot, axis=1)
        back_hidden = cot * prob_in[:, None]
        d_gate = (back_hidden * b * sig * (1.0 + a * (1.0 - sig))).astype(jnp.bfloat16)
        d_up = (back_hidden * a * sig).astype(jnp.bfloat16)
        d_both = jnp.concatenate([d_gate, d_up], 1)
        weighted = (act_low * prob_in[:, None]).astype(jnp.bfloat16)
        terms = [
            jnp.concatenate(
                [
                    contract_rows(rows_in[:, i * half : (i + 1) * half], d_both).astype(jnp.bfloat16),
                    contract_rows(grad_in[:, i * half : (i + 1) * half], weighted).astype(jnp.bfloat16),
                ],
                1,
            )
            for i in range(2)
        ]
        arrived = hop(terms[1], "dp", 1, f"swap{j}")
        block = half // depth
        q = tuple(
            (
                terms[0][kz * block : (kz + 1) * block].astype(jnp.float32)
                + arrived[kz * block : (kz + 1) * block].astype(jnp.float32)
            ).astype(jnp.bfloat16)
            for kz in range(depth)
        )
        sums.append(reduce_line(lax.optimization_barrier(q), depth, f"s{j}"))
        back = [back[i] + contract_last(d_both, both[i][:, : 2 * step]) for i in range(2)]

    route_back = jnp.concatenate(back, 1).astype(jnp.bfloat16)
    parts = [route_back[k * tok_rows : (k + 1) * tok_rows] for k in range(experts)]
    scored = [scores[k * tok_rows : (k + 1) * tok_rows] for k in range(experts)]
    for k in range(1, experts):
        parts[k] = hop(parts[k], "expert", k, f"home{k}")
        scored[k] = hop(scored[k][None], "expert", k, f"score{k}")[0]
    token_sum = parts[0].astype(jnp.float32)
    for k in range(1, experts):
        token_sum = token_sum + parts[k].astype(jnp.float32)
    token_grad = from_local(token_sum.astype(jnp.bfloat16), groups)
    prob_grad = sum(
        jnp.where(routes == (me ^ k), scored[k][:, None], 0.0) for k in range(experts)
    ).astype(jnp.bfloat16)
    weight_grad = jnp.concatenate(
        [s[:, i * step : (i + 1) * step] for i in range(3) for s in sums], 1
    )[None]
    return (token_grad, prob_grad, weight_grad)


def add_low(a, b):
    return (a.astype(jnp.float32) + b.astype(jnp.float32)).astype(jnp.bfloat16)


def kernel(
    own, tok, msk, shares, token_out, score_out, weight_out,
    w, x, m, xt, mt, pb, du, wt, term, swapped, up_in, down_in, sb, hs, hr,
    gs, gr, ps, pr, ds, dr, ws, wr, rs, rr, hsem, hrec,
):
    dp, e = lax.axis_index("dp"), lax.axis_index("expert")
    z, c = dp // 2, dp % 2
    ey, ex = e // 2, e % 2
    near = {1: 2 * ey + 1 - ex, 2: 2 * (1 - ey) + ex, 3: 2 * (1 - ey) + 1 - ex}
    count, rows, cols = own.shape
    step = cols // 3
    toks, width = tok.shape
    partner = z * 2 + 1 - c
    sent = []

    def copy(src, dst, s, r, dev):
        return pltpu.make_async_remote_copy(
            src_ref=src, dst_ref=dst, send_sem=s, recv_sem=r, device_id=dev, device_id_type=MESH
        )

    def send(src, dst, s, r, dev, cond=None):
        d = copy(src, dst, s, r, dev)
        if cond is None:
            d.start()
        else:
            pl.when(cond)(d.start)
        sent.append((cond, d))

    def arrive(dst, s, r, cond=None):
        d = copy(dst, dst, s, r, (partner, e))
        if cond is None:
            d.wait_recv()
        else:
            pl.when(cond)(d.wait_recv)

    barrier = pltpu.get_barrier_semaphore()
    others = [(partner, e)] + [(((z + i) % 4) * 2 + c, e) for i in (1, 2, 3)]
    others += [(dp, near[k]) for k in (1, 2, 3)]
    for dev in others:
        pl.semaphore_signal(barrier, inc=1, device_id=dev, device_id_type=MESH)
    pl.semaphore_wait(barrier, len(others))

    up, down = ((z + 1) * 2 + c, e), ((z - 1) * 2 + c, e)

    def gather_own(j):
        send(own.at[j], w.at[j, dp], gs.at[j, 0, 0], gr.at[j, 0, 0], up, z < 3)
        send(own.at[j], w.at[j, dp], gs.at[j, 1, 0], gr.at[j, 1, 0], down, z > 0)
        send(own.at[j], w.at[j, dp], ps.at[j, z], pr.at[j, z], (partner, e))
        w[j, dp] = own[j]

    def gather_step(j, s):
        for side, has, more, dev in (
            (0, z - 1 - s >= 0, z < 3, up),
            (1, z + 1 + s <= 3, z > 0, down),
        ):
            at = jnp.where(has, z - 1 - s if side == 0 else z + 1 + s, z)
            block = w.at[j, at * 2 + c]
            arrive(block, gs.at[j, side, s], gr.at[j, side, s], has)
            if s < 2:
                send(block, block, gs.at[j, side, s + 1], gr.at[j, side, s + 1], dev, has & more)
            send(block, block, ps.at[j, at], pr.at[j, at], (partner, e), has)

    def pairs_done(j):
        for i in range(4):
            arrive(w.at[j, i * 2 + 1 - c], ps.at[j, i], pr.at[j, i])

    half = toks // 2

    def spread_own(src, dst, at):
        send(src, dst.at[e], ds.at[at], dr.at[at], (dp, near[1]))
        send(src, dst.at[e], ds.at[at + 1], dr.at[at + 1], (dp, near[2]))

    def spread_more(dst, at):
        first, second = pl.ds(0, half), pl.ds(half, half)
        arrive(dst.at[near[1]], ds.at[at], dr.at[at])
        top = dst.at[near[1], first]
        send(top, top, ds.at[at + 2], dr.at[at + 2], (dp, near[2]))
        arrive(dst.at[near[2]], ds.at[at + 1], dr.at[at + 1])
        low = dst.at[near[2], second]
        send(low, low, ds.at[at + 3], dr.at[at + 3], (dp, near[1]))

    def spread_done(dst, at):
        first, second = pl.ds(0, half), pl.ds(half, half)
        arrive(dst.at[near[3], first], ds.at[at + 2], dr.at[at + 2])
        arrive(dst.at[near[3], second], ds.at[at + 3], dr.at[at + 3])

    def forward(j):
        def body(i, _):
            lanes = lax.broadcasted_iota(jnp.int32, (toks, 128), 1)
            p = jnp.sum(jnp.where(lanes == e, pb[i], 0.0), axis=1, keepdims=True)
            part = lambda k: w[j, :, :, k * step : (k + 1) * step].reshape(width, step)
            a, b, cot = dot_f32(x[i], part(0)), dot_f32(x[i], part(1)), dot_f32(m[i], part(2))
            sig = jax.nn.sigmoid(a)
            act = (a * sig * b).astype(jnp.bfloat16).astype(jnp.float32)
            score = jnp.sum(act * cot, axis=1, keepdims=True)
            sb[i] = jnp.broadcast_to(score, (toks, 128)) + (0.0 if j == 0 else sb[i])
            back = cot * p
            here = pl.ds(pl.multiple_of(i * toks, toks), toks)
            du[j, here, :step] = (back * b * sig * (1.0 + a * (1.0 - sig))).astype(jnp.bfloat16)
            du[j, here, step:] = (back * a * sig).astype(jnp.bfloat16)
            wt[here, :] = (act * p).astype(jnp.bfloat16)
            return 0

        lax.fori_loop(0, 4, body, 0)

    def gradient(j):
        def body(i, parity):
            d = i * 2 + parity
            here = pl.ds(pl.multiple_of(d * rows, rows), rows)
            term[j, d, :, : 2 * step] = dot_f32(xt[here, :], du[j]).astype(jnp.bfloat16)
            term[j, d, :, 2 * step :] = dot_f32(mt[here, :], wt[...]).astype(jnp.bfloat16)
            return parity

        lax.fori_loop(0, 4, body, 1 - c)
        for i in range(4):
            send(
                term.at[j, i * 2 + 1 - c], swapped.at[j, i],
                ws.at[j, i], wr.at[j, i], (partner, e),
            )
        lax.fori_loop(0, 4, body, c)

    def reduce_start(j):
        for i in range(4):
            arrive(swapped.at[j, i], ws.at[j, i], wr.at[j, i])
            term[j, i * 2 + c] = add_low(term[j, i * 2 + c], swapped[j, i])
        for r in range(3):
            t = 3 - r
            send(term.at[j, t * 2 + c], up_in.at[j, t], rs.at[j, 0, t], rr.at[j, 0, t], up, z == 0)
            t = r
            send(term.at[j, t * 2 + c], down_in.at[j, t], rs.at[j, 1, t], rr.at[j, 1, t], down, z == 3)

    def reduce_step(j, side, t, at):
        inbox = up_in if side == 0 else down_in
        cond = z == at
        arrive(inbox.at[j, t], rs.at[j, side, t], rr.at[j, side, t], cond)

        @pl.when(cond)
        def _():
            term[j, t * 2 + c] = add_low(term[j, t * 2 + c], inbox[j, t])

        send(
            term.at[j, t * 2 + c], inbox.at[j, t], rs.at[j, side, t], rr.at[j, side, t],
            up if side == 0 else down, cond,
        )

    def reduce_mid(j, r):
        if r == 2:
            reduce_step(j, 0, 3, 2)
            reduce_step(j, 1, 0, 1)
        else:
            reduce_step(j, 0, 3 - r, 1)
            reduce_step(j, 1, r, 2)

    def reduce_end(j):
        arrive(up_in.at[j, z], rs.at[j, 0, z], rr.at[j, 0, z], z > 0)
        arrive(down_in.at[j, z], rs.at[j, 1, z], rr.at[j, 1, z], z < 3)
        edges = ((z == 0, False, True), (z == 3, True, False), ((z > 0) & (z < 3), True, True))
        for cond, low, high in edges:

            @pl.when(cond)
            def _():
                total = term[j, dp].astype(jnp.float32)
                if low:
                    total = total + up_in[j, z].astype(jnp.float32)
                if high:
                    total = total + down_in[j, z].astype(jnp.float32)
                total = total.astype(jnp.bfloat16)
                for k in range(3):
                    at = (k * count + j) * step
                    weight_out[:, at : at + step] = total[:, k * step : (k + 1) * step]

    def home():
        def back(i):
            at = pl.ds(pl.multiple_of(i * toks, toks), toks)
            total = 0.0
            for j in range(count):
                total = total + contract_last(
                    du[j, at, :], w[j, :, :, : 2 * step].reshape(width, 2 * step)
                )
            hs[i] = total.astype(jnp.bfloat16)

        for k in (3, 1, 2):
            send(
                sb.at[near[k]], score_out.at[e],
                hsem.at[2 + k], hrec.at[2 + k], (dp, near[k]),
            )
        score_out[e] = sb[e]

        def each(i, _):
            back(i)
            return 0

        lax.fori_loop(0, 4, each, 0)
        for k in (3, 1, 2):
            send(hs.at[near[k]], hr.at[e], hsem.at[k - 1], hrec.at[k - 1], (dp, near[k]))

    def home_done():
        total = hs[e].astype(jnp.float32)
        for k in (1, 2, 3):
            arrive(hr.at[near[k]], hsem.at[k - 1], hrec.at[k - 1])
            total = total + hr[near[k]].astype(jnp.float32)
            arrive(score_out.at[near[k]], hsem.at[2 + k], hrec.at[2 + k])
        token_out[...] = total.astype(jnp.bfloat16)

    spread_own(tok, x, 0)
    gather_own(0)
    for k in (1, 2, 3):
        send(shares, pb.at[e], ds.at[7 + k], dr.at[7 + k], (dp, near[k]))
    spread_own(msk, m, 4)
    x[e], m[e], pb[e] = tok[...], msk[...], shares[...]
    gather_step(0, 0)
    spread_more(x, 0)
    gather_step(0, 1)
    gather_own(1)
    spread_more(m, 4)
    gather_step(0, 2)
    gather_step(1, 0)
    for k in (1, 2, 3):
        arrive(pb.at[near[k]], ds.at[7 + k], dr.at[7 + k])
    spread_done(x, 0)
    spread_done(m, 4)
    for i in range(4):
        xt[:, i * toks : (i + 1) * toks] = x[i].T
        mt[:, i * toks : (i + 1) * toks] = m[i].T
    pairs_done(0)
    gather_step(1, 1)
    gather_own(2)
    forward(0)
    gradient(0)
    reduce_start(0)
    gather_step(1, 2)
    pairs_done(1)
    gather_step(2, 0)
    forward(1)
    gradient(1)
    reduce_start(1)
    reduce_mid(0, 0)
    gather_step(2, 1)
    reduce_mid(0, 1)
    gather_step(2, 2)
    reduce_mid(0, 2)
    pairs_done(2)
    forward(2)
    gradient(2)
    reduce_start(2)
    reduce_mid(1, 0)
    home()
    reduce_mid(1, 1)
    reduce_mid(1, 2)
    reduce_end(0)
    reduce_mid(2, 0)
    reduce_end(1)
    reduce_mid(2, 1)
    home_done()
    reduce_mid(2, 2)
    reduce_end(2)
    for cond, d in sent:
        if cond is None:
            d.wait_send()
        else:
            pl.when(cond)(d.wait_send)


def per_device_line(
    tokens, out_grad, routes, route_probs, kept_count, gate_weight, up_weight, down_weight
):
    toks, width = tokens.shape
    rows, hidden = gate_weight.shape[1:]
    count, step = 3, hidden // 3
    me = lax.axis_index("expert")
    row = me * toks + jnp.arange(toks, dtype=jnp.int32)
    masked = jnp.where((row < kept_count[0])[:, None], out_grad, jnp.zeros_like(out_grad))
    lanes = jnp.arange(128, dtype=jnp.int32)
    probs = route_probs.astype(jnp.float32)
    shares = sum(
        jnp.where(routes[:, k : k + 1] == lanes[None, :], probs[:, k : k + 1], 0.0)
        for k in range(routes.shape[1])
    )
    own = jnp.stack(
        [
            jnp.concatenate([v[0][:, j * step : (j + 1) * step] for v in (gate_weight, up_weight, down_weight)], 1)
            for j in range(count)
        ]
    )
    cols = 3 * step
    low, full = jnp.bfloat16, jnp.float32
    dma = pltpu.SemaphoreType.DMA
    vmem = pl.BlockSpec(memory_space=pltpu.VMEM)
    token_grad, scores, weight_grad = pl.pallas_call(
        kernel,
        out_shape=(
            jax.ShapeDtypeStruct((toks, width), low),
            jax.ShapeDtypeStruct((4, toks, 128), full),
            jax.ShapeDtypeStruct((rows, 3 * hidden), low),
        ),
        in_specs=[vmem] * 4,
        out_specs=(vmem,) * 3,
        scratch_shapes=[
            pltpu.VMEM((count, 8, rows, cols), low),
            pltpu.VMEM((4, toks, width), low),
            pltpu.VMEM((4, toks, width), low),
            pltpu.VMEM((width, 4 * toks), low),
            pltpu.VMEM((width, 4 * toks), low),
            pltpu.VMEM((4, toks, 128), full),
            pltpu.VMEM((count, 4 * toks, 2 * step), low),
            pltpu.VMEM((4 * toks, step), low),
            pltpu.VMEM((count, 8, rows, cols), low),
            pltpu.VMEM((count, 4, rows, cols), low),
            pltpu.VMEM((count, 4, rows, cols), low),
            pltpu.VMEM((count, 4, rows, cols), low),
            pltpu.VMEM((4, toks, 128), full),
            pltpu.VMEM((4, toks, width), low),
            pltpu.VMEM((4, toks, width), low),
            dma((count, 2, 3)), dma((count, 2, 3)),
            dma((count, 4)), dma((count, 4)),
            dma((11,)), dma((11,)),
            dma((count, 4)), dma((count, 4)),
            dma((count, 2, 4)), dma((count, 2, 4)),
            dma((6,)), dma((6,)),
        ],
        compiler_params=pltpu.CompilerParams(
            collective_id=0, has_side_effects=True, vmem_limit_bytes=67043328
        ),
    )(own, tokens, masked, shares)
    columns = scores[:, :, 0]
    prob_grad = sum(
        jnp.where(routes == i, columns[i][:, None], 0.0) for i in range(4)
    ).astype(jnp.bfloat16)
    return (token_grad, prob_grad, weight_grad[None])


def solution(mesh):
    in_specs = (
        P(("dp", "expert"), None),
        P(("dp", "expert"), None),
        P(("dp", "expert"), None),
        P(("dp", "expert"), None),
        P("dp"),
        P("expert", "dp", None),
        P("expert", "dp", None),
        P("expert", "dp", None),
    )
    out_specs = (P(("dp", "expert"), None), P(("dp", "expert"), None), P("expert", "dp", None))

    line = mesh.shape["dp"] == 4 * CORES and mesh.shape["expert"] == 4
    return jax.shard_map(
        per_device_line if line else per_device,
        mesh=mesh, in_specs=in_specs, out_specs=out_specs, check_vma=False,
    )
```

```python
import jax
import jax.numpy as jnp
from jax import lax
from jax.sharding import PartitionSpec as P
from jax.experimental import pallas as pl
from jax.experimental.pallas import tpu as pltpu

MESH = pl.DeviceIdType.MESH
CORES = 2


def dot_f32(left, right):
    return jnp.dot(left, right, preferred_element_type=jnp.float32)


def contract_rows(left, right):
    return lax.dot_general(
        left, right, (((0,), (0,)), ((), ())), preferred_element_type=jnp.float32
    )


def contract_last(left, right):
    return lax.dot_general(
        left, right, (((1,), (1,)), ((), ())), preferred_element_type=jnp.float32
    )


def hop(x, axis, mask, name):
    size = lax.axis_size(axis)
    with jax.named_scope(name):
        return lax.ppermute(x, axis, [(i, i ^ mask) for i in range(size)])


def z_send(x, moves, name):
    pairs = [(a * CORES + c, b * CORES + c) for a, b in moves for c in range(CORES)]
    with jax.named_scope(name):
        return lax.ppermute(x, "dp", pairs)


def xor_blocks(x, blocks):
    me = lax.axis_index("dp")
    rows, width = x.shape
    size = width // blocks
    depth = blocks // CORES
    parts = [x[:, i * size : (i + 1) * size] for i in range(blocks)]
    bit = 1
    while bit < blocks:
        flip = (me & bit) != 0
        parts = [jnp.where(flip, parts[i ^ bit], parts[i]) for i in range(blocks)]
        bit *= 2
    return parts, depth


def to_local(x, blocks):
    parts, depth = xor_blocks(x, blocks)
    return jnp.concatenate([parts[kz * CORES + kc] for kc in range(CORES) for kz in range(depth)], 1)


def from_local(x, blocks):
    depth = blocks // CORES
    size = x.shape[1] // blocks
    cut = [x[:, i * size : (i + 1) * size] for i in range(blocks)]
    natural = [cut[kc * depth + kz] for kz in range(depth) for kc in range(CORES)]
    parts, _ = xor_blocks(jnp.concatenate(natural, 1), blocks)
    return jnp.concatenate(parts, 1)


def spread(x, experts, name):
    if experts != 4:
        return jnp.concatenate([x] + [hop(x, "expert", k, f"{name}{k}") for k in range(1, experts)], 0)
    half = x.shape[0] // 2
    along_x = hop(x, "expert", 1, f"{name}_x")
    along_y = hop(x, "expert", 2, f"{name}_y")
    top = hop(along_x[:half], "expert", 2, f"{name}_xy")
    bottom = hop(along_y[half:], "expert", 1, f"{name}_yx")
    return jnp.concatenate([x, along_x, along_y, top, bottom], 0)


def reduce_line(q, depth, tag):
    def add(a, b):
        return (a.astype(jnp.float32) + b.astype(jnp.float32)).astype(jnp.bfloat16)

    if depth != 4:
        total = q[0].astype(jnp.float32)
        for kz in range(1, depth):
            total = total + hop(q[kz], "dp", kz * CORES, f"{tag}_{kz}").astype(jnp.float32)
        return total.astype(jnp.bfloat16)
    outer, middle, inner = [(3, 2), (0, 1)], [(2, 1), (1, 2)], [(1, 0), (2, 3)]
    a0 = z_send(q[3], outer, f"{tag}_a0")
    a1 = z_send(q[2], outer, f"{tag}_a1")
    a2 = z_send(q[1], outer, f"{tag}_a2")
    b0 = z_send(add(q[2], a0), middle, f"{tag}_b0")
    b1 = z_send(add(q[3], a1), middle, f"{tag}_b1")
    c0 = z_send(add(q[1], b0), inner, f"{tag}_c0")
    total = q[0].astype(jnp.float32) + a2.astype(jnp.float32)
    return (total + b1.astype(jnp.float32) + c0.astype(jnp.float32)).astype(jnp.bfloat16)


def gather_line(own, depth, tag):
    if depth != 4:
        return jnp.concatenate(
            [own] + [hop(own, "dp", kz * CORES, f"{tag}_{kz}") for kz in range(1, depth)], 0
        )
    z = lax.axis_index("dp") // CORES
    inside = (z == 1) | (z == 2)
    outer, middle, inner = [(3, 2), (0, 1)], [(2, 1), (1, 2)], [(1, 0), (2, 3)]
    o = z_send(own, outer, f"{tag}_o")
    m0 = z_send(own, middle, f"{tag}_m0")
    i0 = z_send(own, inner, f"{tag}_i0")
    m1 = z_send(o, middle, f"{tag}_m1")
    i1 = z_send(m0, inner, f"{tag}_i1")
    i2 = z_send(m1, inner, f"{tag}_i2")
    return jnp.concatenate(
        [own, jnp.where(inside, o, i0), jnp.where(inside, m1, i1), jnp.where(inside, m0, i2)], 0
    )


def chunks_of(hidden):
    return 3 if hidden % 384 == 0 else 1


def per_device(
    tokens, out_grad, routes, route_probs, kept_count, gate_weight, up_weight, down_weight
):
    tok_rows, width = tokens.shape
    experts = lax.axis_size("expert")
    groups = lax.axis_size("dp")
    depth = groups // CORES
    hidden = gate_weight.shape[2]
    count = chunks_of(hidden)
    step = hidden // count
    me = lax.axis_index("expert")

    row = me * tok_rows + jnp.arange(tok_rows, dtype=jnp.int32)
    kept = row < kept_count[0]
    masked = jnp.where(kept[:, None], out_grad, jnp.zeros_like(out_grad))
    probs = route_probs.astype(jnp.float32)

    def share(k):
        return jnp.sum(jnp.where(routes == (me ^ k), probs, 0.0), axis=1)

    prob_in = jnp.concatenate(
        [share(0)] + [hop(share(k)[None], "expert", k, f"prob{k}")[0] for k in range(1, experts)]
    )
    rows_in = spread(to_local(tokens, groups), experts, "rows")
    grad_in = spread(to_local(masked, groups), experts, "grad")

    half = width // CORES
    scores = 0.0
    back = [0.0, 0.0]
    sums = []
    for j in range(count):
        cut = slice(j * step, (j + 1) * step)
        own = jnp.concatenate(
            [gate_weight[0][:, cut], up_weight[0][:, cut], down_weight[0][:, cut]], 1
        )
        mine = gather_line(own, depth, f"g{j}")
        other = hop(mine, "dp", 1, f"pair{j}")
        both = (mine, other)
        pre = sum(dot_f32(rows_in[:, i * half : (i + 1) * half], both[i][:, : 2 * step]) for i in range(2))
        cot = sum(dot_f32(grad_in[:, i * half : (i + 1) * half], both[i][:, 2 * step :]) for i in range(2))
        a, b = pre[:, :step], pre[:, step:]
        sig = jax.nn.sigmoid(a)
        act = a * sig * b
        act_low = act.astype(jnp.bfloat16).astype(jnp.float32)
        scores = scores + jnp.sum(act_low * cot, axis=1)
        back_hidden = cot * prob_in[:, None]
        d_gate = (back_hidden * b * sig * (1.0 + a * (1.0 - sig))).astype(jnp.bfloat16)
        d_up = (back_hidden * a * sig).astype(jnp.bfloat16)
        d_both = jnp.concatenate([d_gate, d_up], 1)
        weighted = (act_low * prob_in[:, None]).astype(jnp.bfloat16)
        terms = [
            jnp.concatenate(
                [
                    contract_rows(rows_in[:, i * half : (i + 1) * half], d_both).astype(jnp.bfloat16),
                    contract_rows(grad_in[:, i * half : (i + 1) * half], weighted).astype(jnp.bfloat16),
                ],
                1,
            )
            for i in range(2)
        ]
        arrived = hop(terms[1], "dp", 1, f"swap{j}")
        block = half // depth
        q = tuple(
            (
                terms[0][kz * block : (kz + 1) * block].astype(jnp.float32)
                + arrived[kz * block : (kz + 1) * block].astype(jnp.float32)
            ).astype(jnp.bfloat16)
            for kz in range(depth)
        )
        sums.append(reduce_line(lax.optimization_barrier(q), depth, f"s{j}"))
        back = [back[i] + contract_last(d_both, both[i][:, : 2 * step]) for i in range(2)]

    route_back = jnp.concatenate(back, 1).astype(jnp.bfloat16)
    parts = [route_back[k * tok_rows : (k + 1) * tok_rows] for k in range(experts)]
    scored = [scores[k * tok_rows : (k + 1) * tok_rows] for k in range(experts)]
    for k in range(1, experts):
        parts[k] = hop(parts[k], "expert", k, f"home{k}")
        scored[k] = hop(scored[k][None], "expert", k, f"score{k}")[0]
    token_sum = parts[0].astype(jnp.float32)
    for k in range(1, experts):
        token_sum = token_sum + parts[k].astype(jnp.float32)
    token_grad = from_local(token_sum.astype(jnp.bfloat16), groups)
    prob_grad = sum(
        jnp.where(routes == (me ^ k), scored[k][:, None], 0.0) for k in range(experts)
    ).astype(jnp.bfloat16)
    weight_grad = jnp.concatenate(
        [s[:, i * step : (i + 1) * step] for i in range(3) for s in sums], 1
    )[None]
    return (token_grad, prob_grad, weight_grad)


def add_low(a, b):
    return (a.astype(jnp.float32) + b.astype(jnp.float32)).astype(jnp.bfloat16)


def kernel(
    gate, up_w, down_w, tok, grad, routes, probs, kept, token_out, prob_out, weight_out,
    w, x, m, xt, mt, pb, du, wt, term, swapped, up_in, down_in, sb, sr, hs, hr,
    gs, gr, ps, pr, ds, dr, ws, wr, rs, rr, hsem, hrec,
):
    dp, e = lax.axis_index("dp"), lax.axis_index("expert")
    z, c = dp // 2, dp % 2
    ey, ex = e // 2, e % 2
    near = {1: 2 * ey + 1 - ex, 2: 2 * (1 - ey) + ex, 3: 2 * (1 - ey) + 1 - ex}
    count, _, rows, cols = w.shape
    step = cols // 3
    toks, width = tok.shape
    partner = z * 2 + 1 - c
    sent = []

    def copy(src, dst, s, r, dev):
        return pltpu.make_async_remote_copy(
            src_ref=src, dst_ref=dst, send_sem=s, recv_sem=r, device_id=dev, device_id_type=MESH
        )

    def send(src, dst, s, r, dev, cond=None):
        d = copy(src, dst, s, r, dev)
        if cond is None:
            d.start()
        else:
            pl.when(cond)(d.start)
        sent.append((cond, d))

    def arrive(dst, s, r, cond=None):
        d = copy(dst, dst, s, r, (partner, e))
        if cond is None:
            d.wait_recv()
        else:
            pl.when(cond)(d.wait_recv)

    barrier = pltpu.get_barrier_semaphore()
    others = [(partner, e)] + [(((z + i) % 4) * 2 + c, e) for i in (1, 2, 3)]
    others += [(dp, near[k]) for k in (1, 2, 3)]
    for dev in others:
        pl.semaphore_signal(barrier, inc=1, device_id=dev, device_id_type=MESH)
    x[e] = tok[...]
    for j in range(count):
        for k, ref in enumerate((gate, up_w, down_w)):
            w[j, dp, :, k * step : (k + 1) * step] = ref[0, :, j * step : (j + 1) * step]
    row = e * toks + lax.broadcasted_iota(jnp.int32, (toks, width), 0)
    m[e] = jnp.where(row < kept[0], grad[...], jnp.zeros((), jnp.bfloat16))
    lanes = lax.broadcasted_iota(jnp.int32, (toks, 128), 1)
    pb[e] = sum(
        jnp.where(routes[:, k : k + 1] == lanes, probs[:, k : k + 1].astype(jnp.float32), 0.0)
        for k in range(routes.shape[1])
    ).astype(jnp.bfloat16)
    pl.semaphore_wait(barrier, len(others))

    up, down = ((z + 1) * 2 + c, e), ((z - 1) * 2 + c, e)

    def gather_own(j):
        send(w.at[j, dp], w.at[j, dp], gs.at[j, 0, 0], gr.at[j, 0, 0], up, z < 3)
        send(w.at[j, dp], w.at[j, dp], gs.at[j, 1, 0], gr.at[j, 1, 0], down, z > 0)
        send(w.at[j, dp], w.at[j, dp], ps.at[j, z], pr.at[j, z], (partner, e))

    def gather_step(j, s):
        for side, has, more, dev in (
            (0, z - 1 - s >= 0, z < 3, up),
            (1, z + 1 + s <= 3, z > 0, down),
        ):
            at = jnp.where(has, z - 1 - s if side == 0 else z + 1 + s, z)
            block = w.at[j, at * 2 + c]
            arrive(block, gs.at[j, side, s], gr.at[j, side, s], has)
            if s < 2:
                send(block, block, gs.at[j, side, s + 1], gr.at[j, side, s + 1], dev, has & more)
            send(block, block, ps.at[j, at], pr.at[j, at], (partner, e), has)

    def pairs_done(j):
        for i in range(4):
            arrive(w.at[j, i * 2 + 1 - c], ps.at[j, i], pr.at[j, i])

    half = toks // 2

    def spread_own(dst, at):
        send(dst.at[e], dst.at[e], ds.at[at], dr.at[at], (dp, near[1]))
        send(dst.at[e], dst.at[e], ds.at[at + 1], dr.at[at + 1], (dp, near[2]))

    def spread_more(dst, at):
        first, second = pl.ds(0, half), pl.ds(half, half)
        arrive(dst.at[near[1]], ds.at[at], dr.at[at])
        top = dst.at[near[1], first]
        send(top, top, ds.at[at + 2], dr.at[at + 2], (dp, near[2]))
        arrive(dst.at[near[2]], ds.at[at + 1], dr.at[at + 1])
        low = dst.at[near[2], second]
        send(low, low, ds.at[at + 3], dr.at[at + 3], (dp, near[1]))

    def spread_done(dst, at):
        first, second = pl.ds(0, half), pl.ds(half, half)
        arrive(dst.at[near[3], first], ds.at[at + 2], dr.at[at + 2])
        arrive(dst.at[near[3], second], ds.at[at + 3], dr.at[at + 3])

    def forward(j, first=0, last=4):
        def body(k, _):
            i = ((ey + k // 2) % 2) * 2 + (ex + k % 2) % 2
            p = pb[i].astype(jnp.float32)
            p = jnp.sum(jnp.where(lanes == e, p, 0.0), axis=1, keepdims=True)
            part = lambda k: w[j, :, :, k * step : (k + 1) * step].reshape(width, step)
            a, b, cot = dot_f32(x[i], part(0)), dot_f32(x[i], part(1)), dot_f32(m[i], part(2))
            sig = jax.nn.sigmoid(a)
            act = (a * sig * b).astype(jnp.bfloat16).astype(jnp.float32)
            score = jnp.sum(act * cot, axis=1, keepdims=True)
            sb[i] = jnp.broadcast_to(score, (toks, 128)) + (0.0 if j == 0 else sb[i])
            back = cot * p
            here = pl.ds(pl.multiple_of(i * toks, toks), toks)
            du[j, here, :step] = (back * b * sig * (1.0 + a * (1.0 - sig))).astype(jnp.bfloat16)
            du[j, here, step:] = (back * a * sig).astype(jnp.bfloat16)
            wt[here, :] = (act * p).astype(jnp.bfloat16)
            if j == 0:
                xt[:, here] = x[i].T
                mt[:, here] = m[i].T
            return 0

        lax.fori_loop(first, last, body, 0)

    def gradient(j):
        def body(i, parity):
            d = i * 2 + parity
            here = pl.ds(pl.multiple_of(d * rows, rows), rows)
            term[j, d, :, : 2 * step] = dot_f32(xt[here, :], du[j]).astype(jnp.bfloat16)
            term[j, d, :, 2 * step :] = dot_f32(mt[here, :], wt[...]).astype(jnp.bfloat16)
            return parity

        lax.fori_loop(0, 4, body, 1 - c)
        for i in range(4):
            send(
                term.at[j, i * 2 + 1 - c], swapped.at[j, i],
                ws.at[j, i], wr.at[j, i], (partner, e),
            )
        lax.fori_loop(0, 4, body, c)

    def reduce_start(j):
        for i in range(4):
            arrive(swapped.at[j, i], ws.at[j, i], wr.at[j, i])
            term[j, i * 2 + c] = add_low(term[j, i * 2 + c], swapped[j, i])
        for r in range(3):
            t = 3 - r
            send(term.at[j, t * 2 + c], up_in.at[j, t], rs.at[j, 0, t], rr.at[j, 0, t], up, z == 0)
            t = r
            send(term.at[j, t * 2 + c], down_in.at[j, t], rs.at[j, 1, t], rr.at[j, 1, t], down, z == 3)

    def reduce_step(j, side, t, at):
        inbox = up_in if side == 0 else down_in
        cond = z == at
        arrive(inbox.at[j, t], rs.at[j, side, t], rr.at[j, side, t], cond)

        @pl.when(cond)
        def _():
            term[j, t * 2 + c] = add_low(term[j, t * 2 + c], inbox[j, t])

        send(
            term.at[j, t * 2 + c], inbox.at[j, t], rs.at[j, side, t], rr.at[j, side, t],
            up if side == 0 else down, cond,
        )

    def reduce_mid(j, r):
        if r == 2:
            reduce_step(j, 0, 3, 2)
            reduce_step(j, 1, 0, 1)
        else:
            reduce_step(j, 0, 3 - r, 1)
            reduce_step(j, 1, r, 2)

    def reduce_end(j):
        arrive(up_in.at[j, z], rs.at[j, 0, z], rr.at[j, 0, z], z > 0)
        arrive(down_in.at[j, z], rs.at[j, 1, z], rr.at[j, 1, z], z < 3)
        edges = ((z == 0, False, True), (z == 3, True, False), ((z > 0) & (z < 3), True, True))
        for cond, low, high in edges:

            @pl.when(cond)
            def _():
                total = term[j, dp].astype(jnp.float32)
                if low:
                    total = total + up_in[j, z].astype(jnp.float32)
                if high:
                    total = total + down_in[j, z].astype(jnp.float32)
                total = total.astype(jnp.bfloat16)
                for k in range(3):
                    at = (k * count + j) * step
                    weight_out[0, :, at : at + step] = total[:, k * step : (k + 1) * step]

    def home():
        def back(i):
            at = pl.ds(pl.multiple_of(i * toks, toks), toks)
            total = 0.0
            for j in range(count):
                total = total + contract_last(
                    du[j, at, :], w[j, :, :, : 2 * step].reshape(width, 2 * step)
                )
            hs[i] = total.astype(jnp.bfloat16)

        for k in (3, 1, 2):
            send(
                sb.at[near[k]], sr.at[e],
                hsem.at[2 + k], hrec.at[2 + k], (dp, near[k]),
            )
        sr[e] = sb[e]

        def each(i, _):
            back(i)
            return 0

        lax.fori_loop(0, 4, each, 0)
        for k in (3, 1, 2):
            send(hs.at[near[k]], hr.at[e], hsem.at[k - 1], hrec.at[k - 1], (dp, near[k]))

    def home_done():
        total = hs[e].astype(jnp.float32)
        for k in (1, 2, 3):
            arrive(hr.at[near[k]], hsem.at[k - 1], hrec.at[k - 1])
            total = total + hr[near[k]].astype(jnp.float32)
            arrive(sr.at[near[k]], hsem.at[2 + k], hrec.at[2 + k])
        token_out[...] = total.astype(jnp.bfloat16)
        top = routes.shape[1]
        prob_out[...] = sum(
            jnp.where(routes[...] == i, sr[i][:, :top], 0.0) for i in range(4)
        ).astype(jnp.bfloat16)

    spread_own(x, 0)
    gather_own(0)
    spread_own(m, 4)
    for k in (1, 2, 3):
        send(pb.at[e], pb.at[e], ds.at[7 + k], dr.at[7 + k], (dp, near[k]))
    gather_step(0, 0)
    spread_more(x, 0)
    gather_step(0, 1)
    gather_own(1)
    spread_more(m, 4)
    gather_step(0, 2)
    for k in (1, 2, 3):
        arrive(pb.at[near[k]], ds.at[7 + k], dr.at[7 + k])
    pairs_done(0)
    forward(0, 0, 3)
    gather_step(1, 0)
    spread_done(x, 0)
    spread_done(m, 4)
    forward(0, 3, 4)
    gather_own(2)
    gradient(0)
    gather_step(1, 1)
    reduce_start(0)
    gather_step(1, 2)
    pairs_done(1)
    gather_step(2, 0)
    forward(1)
    gradient(1)
    reduce_start(1)
    reduce_mid(0, 0)
    gather_step(2, 1)
    reduce_mid(0, 1)
    gather_step(2, 2)
    reduce_mid(0, 2)
    pairs_done(2)
    forward(2)
    gradient(2)
    reduce_start(2)
    reduce_mid(1, 0)
    home()
    reduce_mid(1, 1)
    reduce_mid(1, 2)
    reduce_end(0)
    reduce_mid(2, 0)
    reduce_end(1)
    reduce_mid(2, 1)
    home_done()
    reduce_mid(2, 2)
    reduce_end(2)
    for cond, d in sent:
        if cond is None:
            d.wait_send()
        else:
            pl.when(cond)(d.wait_send)


def per_device_line(
    tokens, out_grad, routes, route_probs, kept_count, gate_weight, up_weight, down_weight
):
    toks, width = tokens.shape
    rows, hidden = gate_weight.shape[1:]
    count, step = 3, hidden // 3
    cols = 3 * step
    low, full = jnp.bfloat16, jnp.float32
    dma = pltpu.SemaphoreType.DMA
    vmem = pl.BlockSpec(memory_space=pltpu.VMEM)
    return pl.pallas_call(
        kernel,
        out_shape=(
            jax.ShapeDtypeStruct((toks, width), low),
            jax.ShapeDtypeStruct(routes.shape, low),
            jax.ShapeDtypeStruct((1, rows, 3 * hidden), low),
        ),
        in_specs=[vmem] * 7 + [pl.BlockSpec(memory_space=pltpu.SMEM)],
        out_specs=(vmem,) * 3,
        scratch_shapes=[
            pltpu.VMEM((count, 8, rows, cols), low),
            pltpu.VMEM((4, toks, width), low),
            pltpu.VMEM((4, toks, width), low),
            pltpu.VMEM((width, 4 * toks), low),
            pltpu.VMEM((width, 4 * toks), low),
            pltpu.VMEM((4, toks, 128), low),
            pltpu.VMEM((count, 4 * toks, 2 * step), low),
            pltpu.VMEM((4 * toks, step), low),
            pltpu.VMEM((count, 8, rows, cols), low),
            pltpu.VMEM((count, 4, rows, cols), low),
            pltpu.VMEM((count, 4, rows, cols), low),
            pltpu.VMEM((count, 4, rows, cols), low),
            pltpu.VMEM((4, toks, 128), full),
            pltpu.VMEM((4, toks, 128), full),
            pltpu.VMEM((4, toks, width), low),
            pltpu.VMEM((4, toks, width), low),
            dma((count, 2, 3)), dma((count, 2, 3)),
            dma((count, 4)), dma((count, 4)),
            dma((11,)), dma((11,)),
            dma((count, 4)), dma((count, 4)),
            dma((count, 2, 4)), dma((count, 2, 4)),
            dma((6,)), dma((6,)),
        ],
        compiler_params=pltpu.CompilerParams(
            collective_id=0, has_side_effects=True, vmem_limit_bytes=67043328
        ),
    )(gate_weight, up_weight, down_weight, tokens, out_grad, routes, route_probs, kept_count)


def solution(mesh):
    in_specs = (
        P(("dp", "expert"), None),
        P(("dp", "expert"), None),
        P(("dp", "expert"), None),
        P(("dp", "expert"), None),
        P("dp"),
        P("expert", "dp", None),
        P("expert", "dp", None),
        P("expert", "dp", None),
    )
    out_specs = (P(("dp", "expert"), None), P(("dp", "expert"), None), P("expert", "dp", None))

    line = mesh.shape["dp"] == 4 * CORES and mesh.shape["expert"] == 4
    return jax.shard_map(
        per_device_line if line else per_device,
        mesh=mesh, in_specs=in_specs, out_specs=out_specs, check_vma=False,
    )
```

```python
import jax
import jax.numpy as jnp
from jax import lax
from jax.sharding import PartitionSpec as P
from jax.experimental import pallas as pl
from jax.experimental.pallas import tpu as pltpu

MESH = pl.DeviceIdType.MESH
CORES = 2


def dot_f32(left, right):
    return jnp.dot(left, right, preferred_element_type=jnp.float32)


def contract_rows(left, right):
    return lax.dot_general(
        left, right, (((0,), (0,)), ((), ())), preferred_element_type=jnp.float32
    )


def contract_last(left, right):
    return lax.dot_general(
        left, right, (((1,), (1,)), ((), ())), preferred_element_type=jnp.float32
    )


def hop(x, axis, mask, name):
    size = lax.axis_size(axis)
    with jax.named_scope(name):
        return lax.ppermute(x, axis, [(i, i ^ mask) for i in range(size)])


def z_send(x, moves, name):
    pairs = [(a * CORES + c, b * CORES + c) for a, b in moves for c in range(CORES)]
    with jax.named_scope(name):
        return lax.ppermute(x, "dp", pairs)


def xor_blocks(x, blocks):
    me = lax.axis_index("dp")
    rows, width = x.shape
    size = width // blocks
    depth = blocks // CORES
    parts = [x[:, i * size : (i + 1) * size] for i in range(blocks)]
    bit = 1
    while bit < blocks:
        flip = (me & bit) != 0
        parts = [jnp.where(flip, parts[i ^ bit], parts[i]) for i in range(blocks)]
        bit *= 2
    return parts, depth


def to_local(x, blocks):
    parts, depth = xor_blocks(x, blocks)
    return jnp.concatenate([parts[kz * CORES + kc] for kc in range(CORES) for kz in range(depth)], 1)


def from_local(x, blocks):
    depth = blocks // CORES
    size = x.shape[1] // blocks
    cut = [x[:, i * size : (i + 1) * size] for i in range(blocks)]
    natural = [cut[kc * depth + kz] for kz in range(depth) for kc in range(CORES)]
    parts, _ = xor_blocks(jnp.concatenate(natural, 1), blocks)
    return jnp.concatenate(parts, 1)


def spread(x, experts, name):
    if experts != 4:
        return jnp.concatenate([x] + [hop(x, "expert", k, f"{name}{k}") for k in range(1, experts)], 0)
    half = x.shape[0] // 2
    along_x = hop(x, "expert", 1, f"{name}_x")
    along_y = hop(x, "expert", 2, f"{name}_y")
    top = hop(along_x[:half], "expert", 2, f"{name}_xy")
    bottom = hop(along_y[half:], "expert", 1, f"{name}_yx")
    return jnp.concatenate([x, along_x, along_y, top, bottom], 0)


def reduce_line(q, depth, tag):
    def add(a, b):
        return (a.astype(jnp.float32) + b.astype(jnp.float32)).astype(jnp.bfloat16)

    if depth != 4:
        total = q[0].astype(jnp.float32)
        for kz in range(1, depth):
            total = total + hop(q[kz], "dp", kz * CORES, f"{tag}_{kz}").astype(jnp.float32)
        return total.astype(jnp.bfloat16)
    outer, middle, inner = [(3, 2), (0, 1)], [(2, 1), (1, 2)], [(1, 0), (2, 3)]
    a0 = z_send(q[3], outer, f"{tag}_a0")
    a1 = z_send(q[2], outer, f"{tag}_a1")
    a2 = z_send(q[1], outer, f"{tag}_a2")
    b0 = z_send(add(q[2], a0), middle, f"{tag}_b0")
    b1 = z_send(add(q[3], a1), middle, f"{tag}_b1")
    c0 = z_send(add(q[1], b0), inner, f"{tag}_c0")
    total = q[0].astype(jnp.float32) + a2.astype(jnp.float32)
    return (total + b1.astype(jnp.float32) + c0.astype(jnp.float32)).astype(jnp.bfloat16)


def gather_line(own, depth, tag):
    if depth != 4:
        return jnp.concatenate(
            [own] + [hop(own, "dp", kz * CORES, f"{tag}_{kz}") for kz in range(1, depth)], 0
        )
    z = lax.axis_index("dp") // CORES
    inside = (z == 1) | (z == 2)
    outer, middle, inner = [(3, 2), (0, 1)], [(2, 1), (1, 2)], [(1, 0), (2, 3)]
    o = z_send(own, outer, f"{tag}_o")
    m0 = z_send(own, middle, f"{tag}_m0")
    i0 = z_send(own, inner, f"{tag}_i0")
    m1 = z_send(o, middle, f"{tag}_m1")
    i1 = z_send(m0, inner, f"{tag}_i1")
    i2 = z_send(m1, inner, f"{tag}_i2")
    return jnp.concatenate(
        [own, jnp.where(inside, o, i0), jnp.where(inside, m1, i1), jnp.where(inside, m0, i2)], 0
    )


def chunks_of(hidden):
    return 3 if hidden % 384 == 0 else 1


def per_device(
    tokens, out_grad, routes, route_probs, kept_count, gate_weight, up_weight, down_weight
):
    tok_rows, width = tokens.shape
    experts = lax.axis_size("expert")
    groups = lax.axis_size("dp")
    depth = groups // CORES
    hidden = gate_weight.shape[2]
    count = chunks_of(hidden)
    step = hidden // count
    me = lax.axis_index("expert")

    row = me * tok_rows + jnp.arange(tok_rows, dtype=jnp.int32)
    kept = row < kept_count[0]
    masked = jnp.where(kept[:, None], out_grad, jnp.zeros_like(out_grad))
    probs = route_probs.astype(jnp.float32)

    def share(k):
        return jnp.sum(jnp.where(routes == (me ^ k), probs, 0.0), axis=1)

    prob_in = jnp.concatenate(
        [share(0)] + [hop(share(k)[None], "expert", k, f"prob{k}")[0] for k in range(1, experts)]
    )
    rows_in = spread(to_local(tokens, groups), experts, "rows")
    grad_in = spread(to_local(masked, groups), experts, "grad")

    half = width // CORES
    scores = 0.0
    back = [0.0, 0.0]
    sums = []
    for j in range(count):
        cut = slice(j * step, (j + 1) * step)
        own = jnp.concatenate(
            [gate_weight[0][:, cut], up_weight[0][:, cut], down_weight[0][:, cut]], 1
        )
        mine = gather_line(own, depth, f"g{j}")
        other = hop(mine, "dp", 1, f"pair{j}")
        both = (mine, other)
        pre = sum(dot_f32(rows_in[:, i * half : (i + 1) * half], both[i][:, : 2 * step]) for i in range(2))
        cot = sum(dot_f32(grad_in[:, i * half : (i + 1) * half], both[i][:, 2 * step :]) for i in range(2))
        a, b = pre[:, :step], pre[:, step:]
        sig = jax.nn.sigmoid(a)
        act = a * sig * b
        act_low = act.astype(jnp.bfloat16).astype(jnp.float32)
        scores = scores + jnp.sum(act_low * cot, axis=1)
        back_hidden = cot * prob_in[:, None]
        d_gate = (back_hidden * b * sig * (1.0 + a * (1.0 - sig))).astype(jnp.bfloat16)
        d_up = (back_hidden * a * sig).astype(jnp.bfloat16)
        d_both = jnp.concatenate([d_gate, d_up], 1)
        weighted = (act_low * prob_in[:, None]).astype(jnp.bfloat16)
        terms = [
            jnp.concatenate(
                [
                    contract_rows(rows_in[:, i * half : (i + 1) * half], d_both).astype(jnp.bfloat16),
                    contract_rows(grad_in[:, i * half : (i + 1) * half], weighted).astype(jnp.bfloat16),
                ],
                1,
            )
            for i in range(2)
        ]
        arrived = hop(terms[1], "dp", 1, f"swap{j}")
        block = half // depth
        q = tuple(
            (
                terms[0][kz * block : (kz + 1) * block].astype(jnp.float32)
                + arrived[kz * block : (kz + 1) * block].astype(jnp.float32)
            ).astype(jnp.bfloat16)
            for kz in range(depth)
        )
        sums.append(reduce_line(lax.optimization_barrier(q), depth, f"s{j}"))
        back = [back[i] + contract_last(d_both, both[i][:, : 2 * step]) for i in range(2)]

    route_back = jnp.concatenate(back, 1).astype(jnp.bfloat16)
    parts = [route_back[k * tok_rows : (k + 1) * tok_rows] for k in range(experts)]
    scored = [scores[k * tok_rows : (k + 1) * tok_rows] for k in range(experts)]
    for k in range(1, experts):
        parts[k] = hop(parts[k], "expert", k, f"home{k}")
        scored[k] = hop(scored[k][None], "expert", k, f"score{k}")[0]
    token_sum = parts[0].astype(jnp.float32)
    for k in range(1, experts):
        token_sum = token_sum + parts[k].astype(jnp.float32)
    token_grad = from_local(token_sum.astype(jnp.bfloat16), groups)
    prob_grad = sum(
        jnp.where(routes == (me ^ k), scored[k][:, None], 0.0) for k in range(experts)
    ).astype(jnp.bfloat16)
    weight_grad = jnp.concatenate(
        [s[:, i * step : (i + 1) * step] for i in range(3) for s in sums], 1
    )[None]
    return (token_grad, prob_grad, weight_grad)


def add_low(a, b):
    return (a.astype(jnp.float32) + b.astype(jnp.float32)).astype(jnp.bfloat16)


def kernel(
    gate, up_w, down_w, tok, grad, routes, probs, kept, token_out, prob_out, weight_out,
    w, x, m, xt, mt, pb, du, wt, term, swapped, up_in, down_in, sb, sr, hs, hr,
    gs, gr, ps, pr, ds, dr, ws, wr, rs, rr, hsem, hrec,
):
    dp, e = lax.axis_index("dp"), lax.axis_index("expert")
    z, c = dp // 2, dp % 2
    ey, ex = e // 2, e % 2
    near = {1: 2 * ey + 1 - ex, 2: 2 * (1 - ey) + ex, 3: 2 * (1 - ey) + 1 - ex}
    count, _, rows, cols = w.shape
    step = cols // 3
    toks, width = tok.shape
    partner = z * 2 + 1 - c
    sent = []

    def copy(src, dst, s, r, dev):
        return pltpu.make_async_remote_copy(
            src_ref=src, dst_ref=dst, send_sem=s, recv_sem=r, device_id=dev, device_id_type=MESH
        )

    def send(src, dst, s, r, dev, cond=None):
        d = copy(src, dst, s, r, dev)
        if cond is None:
            d.start()
        else:
            pl.when(cond)(d.start)
        sent.append((cond, d))

    def arrive(dst, s, r, cond=None):
        d = copy(dst, dst, s, r, (partner, e))
        if cond is None:
            d.wait_recv()
        else:
            pl.when(cond)(d.wait_recv)

    barrier = pltpu.get_barrier_semaphore()
    others = [(partner, e)] + [(((z + i) % 4) * 2 + c, e) for i in (1, 2, 3)]
    others += [(dp, near[k]) for k in (1, 2, 3)]
    for dev in others:
        pl.semaphore_signal(barrier, inc=1, device_id=dev, device_id_type=MESH)
    x[e] = tok[...]
    for j in range(count):
        for k, ref in enumerate((gate, up_w, down_w)):
            w[j, dp, :, k * step : (k + 1) * step] = ref[0, :, j * step : (j + 1) * step]
    row = e * toks + lax.broadcasted_iota(jnp.int32, (toks, width), 0)
    m[e] = jnp.where(row < kept[0], grad[...], jnp.zeros((), jnp.bfloat16))
    lanes = lax.broadcasted_iota(jnp.int32, (toks, 128), 1)
    def tall(ref, k):
        return jnp.broadcast_to(ref[k : k + 1, :].astype(jnp.float32), (128, toks)).T

    pb[e] = sum(
        jnp.where(tall(routes, k) == lanes.astype(jnp.float32), tall(probs, k), 0.0)
        for k in range(routes.shape[0])
    ).astype(jnp.bfloat16)
    pl.semaphore_wait(barrier, len(others))

    up, down = ((z + 1) * 2 + c, e), ((z - 1) * 2 + c, e)

    def gather_ends(j):
        send(w.at[j, dp], w.at[j, dp], gs.at[j, 0, 0], gr.at[j, 0, 0], up, z == 0)
        send(w.at[j, dp], w.at[j, dp], gs.at[j, 1, 0], gr.at[j, 1, 0], down, z == 3)

    def gather_own(j):
        between = (z > 0) & (z < 3)
        send(w.at[j, dp], w.at[j, dp], gs.at[j, 0, 0], gr.at[j, 0, 0], up, between)
        send(w.at[j, dp], w.at[j, dp], gs.at[j, 1, 0], gr.at[j, 1, 0], down, between)
        send(w.at[j, dp], w.at[j, dp], ps.at[j, z], pr.at[j, z], (partner, e))

    def gather_step(j, s):
        for side, has, more, dev in (
            (0, z - 1 - s >= 0, z < 3, up),
            (1, z + 1 + s <= 3, z > 0, down),
        ):
            at = jnp.where(has, z - 1 - s if side == 0 else z + 1 + s, z)
            block = w.at[j, at * 2 + c]
            arrive(block, gs.at[j, side, s], gr.at[j, side, s], has)
            if s < 2:
                send(block, block, gs.at[j, side, s + 1], gr.at[j, side, s + 1], dev, has & more)
            send(block, block, ps.at[j, at], pr.at[j, at], (partner, e), has)

    def pairs_done(j):
        for i in range(4):
            arrive(w.at[j, i * 2 + 1 - c], ps.at[j, i], pr.at[j, i])

    half = toks // 2

    def spread_own(dst, at):
        send(dst.at[e], dst.at[e], ds.at[at], dr.at[at], (dp, near[1]))
        send(dst.at[e], dst.at[e], ds.at[at + 1], dr.at[at + 1], (dp, near[2]))

    def spread_more(dst, at):
        first, second = pl.ds(0, half), pl.ds(half, half)
        arrive(dst.at[near[1]], ds.at[at], dr.at[at])
        top = dst.at[near[1], first]
        send(top, top, ds.at[at + 2], dr.at[at + 2], (dp, near[2]))
        arrive(dst.at[near[2]], ds.at[at + 1], dr.at[at + 1])
        low = dst.at[near[2], second]
        send(low, low, ds.at[at + 3], dr.at[at + 3], (dp, near[1]))

    def spread_done(dst, at):
        first, second = pl.ds(0, half), pl.ds(half, half)
        arrive(dst.at[near[3], first], ds.at[at + 2], dr.at[at + 2])
        arrive(dst.at[near[3], second], ds.at[at + 3], dr.at[at + 3])

    def forward(j, first=0, last=4):
        def body(k, _):
            i = ((ey + k // 2) % 2) * 2 + (ex + k % 2) % 2
            p = pb[i].astype(jnp.float32)
            p = jnp.sum(jnp.where(lanes == e, p, 0.0), axis=1, keepdims=True)
            part = lambda k: w[j, :, :, k * step : (k + 1) * step].reshape(width, step)
            a, b, cot = dot_f32(x[i], part(0)), dot_f32(x[i], part(1)), dot_f32(m[i], part(2))
            sig = jax.nn.sigmoid(a)
            act = (a * sig * b).astype(jnp.bfloat16).astype(jnp.float32)
            score = jnp.sum(act * cot, axis=1, keepdims=True)
            sb[i] = jnp.broadcast_to(score, (toks, 128)) + (0.0 if j == 0 else sb[i])
            back = cot * p
            here = pl.ds(pl.multiple_of(i * toks, toks), toks)
            du[j, here, :step] = (back * b * sig * (1.0 + a * (1.0 - sig))).astype(jnp.bfloat16)
            du[j, here, step:] = (back * a * sig).astype(jnp.bfloat16)
            wt[here, :] = (act * p).astype(jnp.bfloat16)
            if j == 0:
                xt[:, here] = x[i].T
                mt[:, here] = m[i].T
            return 0

        lax.fori_loop(first, last, body, 0)

    def gradient(j):
        def body(i, parity):
            d = i * 2 + parity
            here = pl.ds(pl.multiple_of(d * rows, rows), rows)
            term[j, d, :, : 2 * step] = dot_f32(xt[here, :], du[j]).astype(jnp.bfloat16)
            term[j, d, :, 2 * step :] = dot_f32(mt[here, :], wt[...]).astype(jnp.bfloat16)
            return parity

        lax.fori_loop(0, 4, body, 1 - c)
        for i in range(4):
            send(
                term.at[j, i * 2 + 1 - c], swapped.at[j, i],
                ws.at[j, i], wr.at[j, i], (partner, e),
            )
        lax.fori_loop(0, 4, body, c)

    def reduce_start(j):
        for i in range(4):
            arrive(swapped.at[j, i], ws.at[j, i], wr.at[j, i])
            term[j, i * 2 + c] = add_low(term[j, i * 2 + c], swapped[j, i])
        for r in range(3):
            t = 3 - r
            send(term.at[j, t * 2 + c], up_in.at[j, t], rs.at[j, 0, t], rr.at[j, 0, t], up, z == 0)
            t = r
            send(term.at[j, t * 2 + c], down_in.at[j, t], rs.at[j, 1, t], rr.at[j, 1, t], down, z == 3)

    def reduce_step(j, side, t, at):
        inbox = up_in if side == 0 else down_in
        cond = z == at
        arrive(inbox.at[j, t], rs.at[j, side, t], rr.at[j, side, t], cond)

        @pl.when(cond)
        def _():
            term[j, t * 2 + c] = add_low(term[j, t * 2 + c], inbox[j, t])

        send(
            term.at[j, t * 2 + c], inbox.at[j, t], rs.at[j, side, t], rr.at[j, side, t],
            up if side == 0 else down, cond,
        )

    def reduce_mid(j, r):
        if r == 2:
            reduce_step(j, 0, 3, 2)
            reduce_step(j, 1, 0, 1)
        else:
            reduce_step(j, 0, 3 - r, 1)
            reduce_step(j, 1, r, 2)

    def reduce_end(j):
        arrive(up_in.at[j, z], rs.at[j, 0, z], rr.at[j, 0, z], z > 0)
        arrive(down_in.at[j, z], rs.at[j, 1, z], rr.at[j, 1, z], z < 3)
        edges = ((z == 0, False, True), (z == 3, True, False), ((z > 0) & (z < 3), True, True))
        for cond, low, high in edges:

            @pl.when(cond)
            def _():
                total = term[j, dp].astype(jnp.float32)
                if low:
                    total = total + up_in[j, z].astype(jnp.float32)
                if high:
                    total = total + down_in[j, z].astype(jnp.float32)
                total = total.astype(jnp.bfloat16)
                for k in range(3):
                    at = (k * count + j) * step
                    weight_out[0, :, at : at + step] = total[:, k * step : (k + 1) * step]

    def home():
        def back(i):
            at = pl.ds(pl.multiple_of(i * toks, toks), toks)
            total = 0.0
            for j in range(count):
                total = total + contract_last(
                    du[j, at, :], w[j, :, :, : 2 * step].reshape(width, 2 * step)
                )
            hs[i] = total.astype(jnp.bfloat16)

        for k in (3, 1, 2):
            send(
                sb.at[near[k]], sr.at[e],
                hsem.at[2 + k], hrec.at[2 + k], (dp, near[k]),
            )
        sr[e] = sb[e]

        def each(i, _):
            back(i)
            return 0

        lax.fori_loop(0, 4, each, 0)
        for k in (3, 1, 2):
            send(hs.at[near[k]], hr.at[e], hsem.at[k - 1], hrec.at[k - 1], (dp, near[k]))

    def home_done():
        total = hs[e].astype(jnp.float32)
        for k in (1, 2, 3):
            arrive(hr.at[near[k]], hsem.at[k - 1], hrec.at[k - 1])
            total = total + hr[near[k]].astype(jnp.float32)
            arrive(sr.at[near[k]], hsem.at[2 + k], hrec.at[2 + k])
        token_out[...] = total.astype(jnp.bfloat16)
        top = routes.shape[0]
        prob_out[...] = sum(
            jnp.where(routes[...] == i, sr[i].T[:top, :], 0.0) for i in range(4)
        ).astype(jnp.bfloat16)

    spread_own(x, 0)
    gather_ends(0)
    gather_own(0)
    gather_ends(1)
    gather_ends(2)
    spread_own(m, 4)
    for k in (1, 2, 3):
        send(pb.at[e], pb.at[e], ds.at[7 + k], dr.at[7 + k], (dp, near[k]))
    gather_step(0, 0)
    spread_more(x, 0)
    gather_step(0, 1)
    gather_own(1)
    spread_more(m, 4)
    gather_step(0, 2)
    for k in (1, 2, 3):
        arrive(pb.at[near[k]], ds.at[7 + k], dr.at[7 + k])
    pairs_done(0)
    forward(0, 0, 3)
    gather_step(1, 0)
    spread_done(x, 0)
    spread_done(m, 4)
    forward(0, 3, 4)
    gather_own(2)
    gradient(0)
    gather_step(1, 1)
    reduce_start(0)
    gather_step(1, 2)
    pairs_done(1)
    gather_step(2, 0)
    forward(1)
    gradient(1)
    reduce_start(1)
    reduce_mid(0, 0)
    gather_step(2, 1)
    reduce_mid(0, 1)
    gather_step(2, 2)
    reduce_mid(0, 2)
    pairs_done(2)
    forward(2)
    gradient(2)
    reduce_start(2)
    reduce_mid(1, 0)
    home()
    reduce_mid(1, 1)
    reduce_mid(1, 2)
    reduce_end(0)
    reduce_mid(2, 0)
    reduce_end(1)
    reduce_mid(2, 1)
    home_done()
    reduce_mid(2, 2)
    reduce_end(2)
    for cond, d in sent:
        if cond is None:
            d.wait_send()
        else:
            pl.when(cond)(d.wait_send)


def per_device_line(
    tokens, out_grad, routes, route_probs, kept_count, gate_weight, up_weight, down_weight
):
    toks, width = tokens.shape
    rows, hidden = gate_weight.shape[1:]
    count, step = 3, hidden // 3
    cols = 3 * step
    low, full = jnp.bfloat16, jnp.float32
    dma = pltpu.SemaphoreType.DMA
    vmem = pl.BlockSpec(memory_space=pltpu.VMEM)
    token_grad, prob_grad, weight_grad = pl.pallas_call(
        kernel,
        out_shape=(
            jax.ShapeDtypeStruct((toks, width), low),
            jax.ShapeDtypeStruct(routes.shape[::-1], low),
            jax.ShapeDtypeStruct((1, rows, 3 * hidden), low),
        ),
        in_specs=[vmem] * 7 + [pl.BlockSpec(memory_space=pltpu.SMEM)],
        out_specs=(vmem,) * 3,
        scratch_shapes=[
            pltpu.VMEM((count, 8, rows, cols), low),
            pltpu.VMEM((4, toks, width), low),
            pltpu.VMEM((4, toks, width), low),
            pltpu.VMEM((width, 4 * toks), low),
            pltpu.VMEM((width, 4 * toks), low),
            pltpu.VMEM((4, toks, 128), low),
            pltpu.VMEM((count, 4 * toks, 2 * step), low),
            pltpu.VMEM((4 * toks, step), low),
            pltpu.VMEM((count, 8, rows, cols), low),
            pltpu.VMEM((count, 4, rows, cols), low),
            pltpu.VMEM((count, 4, rows, cols), low),
            pltpu.VMEM((count, 4, rows, cols), low),
            pltpu.VMEM((4, toks, 128), full),
            pltpu.VMEM((4, toks, 128), full),
            pltpu.VMEM((4, toks, width), low),
            pltpu.VMEM((4, toks, width), low),
            dma((count, 2, 3)), dma((count, 2, 3)),
            dma((count, 4)), dma((count, 4)),
            dma((11,)), dma((11,)),
            dma((count, 4)), dma((count, 4)),
            dma((count, 2, 4)), dma((count, 2, 4)),
            dma((6,)), dma((6,)),
        ],
        compiler_params=pltpu.CompilerParams(
            collective_id=0, has_side_effects=True, vmem_limit_bytes=67043328
        ),
    )(
        gate_weight, up_weight, down_weight, tokens, out_grad, routes.T, route_probs.T, kept_count
    )
    return (token_grad, prob_grad.T, weight_grad)


def solution(mesh):
    in_specs = (
        P(("dp", "expert"), None),
        P(("dp", "expert"), None),
        P(("dp", "expert"), None),
        P(("dp", "expert"), None),
        P("dp"),
        P("expert", "dp", None),
        P("expert", "dp", None),
        P("expert", "dp", None),
    )
    out_specs = (P(("dp", "expert"), None), P(("dp", "expert"), None), P("expert", "dp", None))

    line = mesh.shape["dp"] == 4 * CORES and mesh.shape["expert"] == 4
    return jax.shard_map(
        per_device_line if line else per_device,
        mesh=mesh, in_specs=in_specs, out_specs=out_specs, check_vma=False,
    )
```
